32 devices in a mesh: grp: 2 (over y), head: 4 (over z), tm: 4 (over x, core).
Axes of the slice: x: 2, y: 2, z: 4, core: 2. Of those that a mesh axis runs over, the one named last changes fastest.
Arguments:
- query_rows: bfloat16 [32, 64, 3072], P(('grp', 'tm'), 'head'), parts along dimension 0, may hold values from -180 to 180
- key_rows: bfloat16 [32, 64, 3072], P(('grp', 'tm'), 'head'), parts along dimension 0, may hold values from -6 to 6
- value_rows: bfloat16 [32, 64, 3072], P(('grp', 'tm'), 'head'), parts along dimension 0, may hold values from -6 to 6
- pair_list: int32 [32, 32], P('grp'), parts along dimension 0, may hold values from 0 to 15, as said below
- block_tokens: int32 [32], P('grp'), parts along dimension 0, may hold values from 1 to 64, 768 in all
Outputs:
- attended: bfloat16 [32, 64, 3072], P(('grp', 'tm'), 'head'), parts along dimension 0
The draws below stay inside these ranges and needn't reach their ends.
There are 2 independent parts, one for each index of `grp`. The reference program is written for one: setup_inputs(seed, part) draws one part's arguments, and reference() takes and returns one part's arrays. A program takes and returns all parts, laid end to end along the dimension named above; each array names one. Nothing has to cross between parts.
Inputs may be any that keep to these rules, and one draw needn't show every extreme that they name: `pair_list`: row q names q in column 0 and q xor 1 in column 1; a block may be named twice in a row. The query blocks of one time shard name at most 2 different blocks of a time shard beside it and at most 1 of a time shard two or more away; both bounds are reached.
All inputs are finite; a program needn't handle non-finite values.
Results may differ from the reference program's by a relative error of at most 0.0012.
The reference program's roundings to bfloat16 on the way (of `query_rot`, `key_rot`, `value_rot` and `weights_half`) count: a program that leaves them out, or rounds other values in their place, can miss the bound.
Values may be sent and summed in bfloat16 or wider, within the bound.
A program may use at most 128 MiB of HBM per device.

```python
import math
import jax
import jax.numpy as jnp
import numpy as np
from jax import lax

HEADS = 24
HD = 128
BLK = 64
KPB = 32
NB_DEV = 4
NBLK = 16


def attention_inputs(key):
    base_key = jax.random.fold_in(key, 31)
    query_seed, key_seed = jax.random.split(base_key)
    query_all = jnp.clip(jax.random.normal(query_seed, (NBLK, BLK, HEADS, HD), jnp.float32), -6.0, 6.0)
    key_all = jnp.clip(jax.random.normal(key_seed, (NBLK, BLK, HEADS, HD), jnp.float32), -6.0, 6.0)
    return (query_all.reshape(NBLK, BLK, HEADS * HD), key_all.reshape(NBLK, BLK, HEADS * HD))


def draw_query_rows(key, part):
    return attention_inputs(key)[0].astype(jnp.bfloat16)


def draw_key_rows(key, part):
    return attention_inputs(key)[1].astype(jnp.bfloat16)


def draw_pair_list(key, part):
    seeds = jax.random.split(jax.random.fold_in(key, 47), 8)
    shards = NBLK // NB_DEV
    blocks = jnp.arange(NBLK, dtype=jnp.int32)
    owner = blocks // NB_DEV
    inside = blocks % NB_DEV
    first_pick = jax.random.randint(seeds[0], (shards, shards), 0, NB_DEV)
    step_pick = jax.random.randint(seeds[1], (shards, shards), 1, NB_DEV)
    second_pick = (first_pick + step_pick) % NB_DEV
    far_pick = jax.random.randint(seeds[2], (shards, shards), 0, NB_DEV)
    offsets = jax.random.randint(seeds[3], (NBLK, KPB - 12), -3, 4)
    local_cols = owner[:, None] * NB_DEV + jnp.clip(inside[:, None] + offsets, 0, NB_DEV - 1)
    upper = jnp.where(owner + 1 < shards, owner + 1, owner - 1)
    lower = jnp.where(owner >= 1, owner - 1, owner + 1)
    up_col = upper * NB_DEV + jnp.where(inside % 2 == 0, first_pick[owner, upper], second_pick[owner, upper])
    coin_flip = jax.random.randint(seeds[4], (NBLK,), 0, 2)
    low_col = lower * NB_DEV + jnp.where(coin_flip == 0, first_pick[owner, lower], second_pick[owner, lower])
    span_top = max(shards - 2, 1)
    dist_first = jax.random.randint(seeds[5], (NBLK, 8), 0, span_top)
    dist_second = jax.random.randint(seeds[6], (NBLK, 8), 0, span_top)
    reach = 2 + jnp.minimum(dist_first, dist_second)
    side_sign = jax.random.randint(seeds[7], (NBLK, 8), 0, 2) * 2 - 1
    target = owner[:, None] + side_sign * reach
    target = jnp.where((target >= 0) & (target < shards), target, owner[:, None] - side_sign * reach)
    usable = (target >= 0) & (target < shards)
    safe_target = jnp.clip(target, 0, shards - 1)
    owner_wide = jnp.broadcast_to(owner[:, None], (NBLK, 8))
    far_cols = jnp.where(usable, safe_target * NB_DEV + far_pick[owner_wide, safe_target], blocks[:, None])
    columns = [blocks[:, None], (blocks ^ 1)[:, None], local_cols, up_col[:, None], low_col[:, None], far_cols]
    return jnp.concatenate(columns, axis=1).astype(jnp.int32)


def block_levels(rng, extent, cuts, least, high):
    factor_of, own = 1.0, jax.random.fold_in(rng, 6)
    for axis_at, blocks in cuts:
        draws = jnp.exp(jax.random.uniform(jax.random.fold_in(own, axis_at), (blocks,), jnp.float32, least / len(cuts), high / len(cuts)))
        factor_of = factor_of * jnp.repeat(draws, extent[axis_at] // blocks).reshape([-1 if axis == axis_at else 1 for axis in range(len(extent))])
    return factor_of


def length_profile(number_of, total, most, skew):
    weights = [(1 << 20) // math.isqrt(rank ** skew) + 1 for rank in range(2, number_of + 1)]
    rest, holding = total - most - (number_of - 1), [1] * (number_of - 1)
    while rest > 0:
        candidates = [i for i in range(number_of - 1) if holding[i] < most]
        pool, budget = sum([weights[i] for i in candidates]), rest
        for i in candidates:
            extra = min(most - holding[i], max(1, budget * weights[i] // pool), rest)
            holding[i] = holding[i] + extra
            rest = rest - extra
    return np.array([most] + holding)


def ragged(own_key, count, total, bound, slope):
    if count == 2:
        one = jax.random.randint(own_key, (), max(1, total - bound), min(bound, total - 1) + 1)
        return jnp.stack([one, total - one])
    sizes = jnp.asarray(length_profile(count, total, bound, slope), jnp.int32)
    couples = (count - 1) // 2
    donor, receiver = sizes[1:1 + 2 * couples:2], sizes[2:2 + 2 * couples:2]
    margin = jnp.minimum(donor - 1, bound - receiver)
    moved = jax.random.randint(jax.random.fold_in(own_key, 1), (couples,), 0, 1 << 20) % (margin + 1)
    sizes = sizes.at[1:1 + 2 * couples:2].set(donor - moved).at[2:2 + 2 * couples:2].set(receiver + moved)
    return sizes[jax.random.permutation(jax.random.fold_in(own_key, 2), count)]


def bell_draw(own_key, dims, deviation, most, cuts=(), held_as=jnp.bfloat16):
    drawn = jax.random.normal(own_key, dims, jnp.float32) * deviation
    if len(cuts) > 0:
        drawn = block_levels(own_key, dims, cuts, -0.22, 0.18) * drawn
    return jnp.clip(drawn, min=-most, max=most).astype(held_as)


def setup_inputs(seed: int = 0, part: int = 0) -> dict:
    key_list = jax.random.split(jax.random.key(seed), 6)
    part_keys = jax.random.split(jax.random.fold_in(key_list[5], part), 6)
    query_rows = draw_query_rows(jax.random.fold_in(jax.random.fold_in(key_list[5], part), 71), part)
    key_rows = draw_key_rows(jax.random.fold_in(jax.random.fold_in(key_list[5], part), 71), part)
    value_rows = bell_draw(part_keys[2], (NBLK, BLK, HEADS * HD), 1.0, 6.0, ((0, 4), (1, 4)))
    pair_list = draw_pair_list(jax.random.fold_in(jax.random.fold_in(key_list[5], part), 71), part)
    block_tokens = ragged(part_keys[4], NBLK, NBLK * BLK * 3 // 4, BLK, 2).astype(jnp.int32)
    return {"query_rows": query_rows, "key_rows": key_rows, "value_rows": value_rows, "pair_list": pair_list, "block_tokens": block_tokens}


def sign_table(dimension):
    indices = jnp.arange(dimension, dtype=jnp.int32)
    common = indices[:, None] & indices[None, :]
    parity = jnp.zeros((dimension, dimension), jnp.int32)
    for bit_level in range(dimension.bit_length() - 1):
        parity = parity + (common >> bit_level & 1)
    return jnp.where(parity % 2 == 0, 1.0, -1.0).astype(jnp.float32)

def reference(query_rows, key_rows, value_rows, pair_list, block_tokens):
    sign_rows = sign_table(HD)
    sign_half = sign_rows.astype(jnp.bfloat16)
    rotate_scale = 1.0 / math.sqrt(HD)
    score_scale = 1.0 / math.sqrt(HD)

    def rotate(source):
        flattened = source.reshape(-1, HD)
        turned = jnp.dot(flattened, sign_half, preferred_element_type=jnp.float32) * rotate_scale
        return turned.astype(jnp.bfloat16).reshape(NBLK, BLK, HEADS, HD)
    query_rot = rotate(query_rows)
    key_rot = rotate(key_rows)
    value_rot = rotate(value_rows)
    positions = jnp.arange(BLK, dtype=jnp.int32)
    live_keys = positions[None, :] < block_tokens[:, None]
    earlier = jnp.arange(KPB)[:, None] > jnp.arange(KPB)[None, :]

    def one_block(block_id):
        listed = pair_list[block_id]
        repeated = jnp.any((listed[:, None] == listed[None, :]) & earlier, axis=1)
        key_keep = (live_keys[listed] & ~repeated[:, None]).reshape(KPB * BLK)
        key_block = key_rot[listed].reshape(KPB * BLK, HEADS, HD).astype(jnp.float32)
        value_block = value_rot[listed].reshape(KPB * BLK, HEADS, HD).astype(jnp.float32)
        query_block = query_rot[block_id].astype(jnp.float32)
        scores = jnp.einsum('qhd,khd->hqk', query_block, key_block) * score_scale
        scores = jnp.where(key_keep[None, None, :], scores, -1e+30)
        row_peak = lax.optimization_barrier(jnp.max(scores, axis=-1, keepdims=True))
        weights = jnp.exp(scores - row_peak)
        denominator = lax.optimization_barrier(jnp.sum(weights, axis=-1))
        weights_half = lax.optimization_barrier(weights.astype(jnp.bfloat16)).astype(jnp.float32)
        mixed_rows = jnp.einsum('hqk,khd->qhd', weights_half, value_block)
        mixed_rows = mixed_rows / jnp.transpose(denominator)[:, :, None]
        turned = jnp.dot(mixed_rows.reshape(-1, HD), sign_rows, precision=lax.Precision.HIGHEST) * rotate_scale
        turned = turned.reshape(BLK, HEADS * HD)
        live_rows = positions[:, None] < block_tokens[block_id]
        return jnp.where(live_rows, turned, 0.0).astype(jnp.bfloat16)
    return lax.map(one_block, jnp.arange(NBLK, dtype=jnp.int32))
```

```python
import functools
import math

import jax
import jax.numpy as jnp
from jax import lax
from jax.experimental import pallas as pl
from jax.experimental.pallas import tpu as pltpu
from jax.sharding import PartitionSpec as P

HD = 128
NEAR_CAP = 2
FAR_CAP = 1
LANES = 128
PAIR_HEADS = 3
QUERY_HEADS = 1
MESH = pl.DeviceIdType.MESH


def incoming_slots(count_tm):
    slots = []
    for offset in range(1, count_tm):
        capacity = NEAR_CAP if offset in (1, count_tm - 1) else FAR_CAP
        slots += [(offset, place) for place in range(capacity)]
    return slots


def partner(index, offset, count):
    if count & (count - 1):
        return lax.rem(index + offset, count)
    for level in range(count.bit_length() - 1):
        if offset >> level & 1:
            bit = lax.rem(lax.div(index, 1 << level), 2)
            index = index + (1 << level) * (1 - 2 * bit)
    return index


def heads_together(heads, most):
    return max(size for size in range(1, most + 1) if heads % size == 0)


def sending_order(count):
    order, top = [], 1
    while top < count:
        order = list(range(top, min(2 * top, count))) + order
        top *= 2
    return order


def sign_table(dimension):
    rows = lax.broadcasted_iota(jnp.int32, (dimension, dimension), 0)
    columns = lax.broadcasted_iota(jnp.int32, (dimension, dimension), 1)
    common = rows & columns
    parity = jnp.zeros((dimension, dimension), jnp.int32)
    for bit_level in range(dimension.bit_length() - 1):
        parity = parity + ((common >> bit_level) & 1)
    return jnp.where((parity & 1) == 0, 1.0, -1.0).astype(jnp.float32)


def kernel(
    sizes,
    query_ref,
    key_ref,
    value_ref,
    pair_ref,
    tokens_far,
    out_ref,
    pair_in,
    query_in,
    store,
    outbox,
    staged,
    pair_here,
    tokens_ref,
    listed_ref,
    place_ref,
    wanted_ref,
    bias_ref,
    sign_ref,
    pair_send,
    pair_recv,
    query_send,
    query_recv,
    pair_local,
    query_local,
    entered_low,
    entered_high,
    halo_send,
    halo_recv,
    back_send,
    back_recv,
    back_local,
    pair_sem,
    tokens_sem,
):
    count_head, count_tm, blocks, part, heads, block, total_blocks, slots, padded, grouped = sizes
    pair_heads, query_heads = grouped
    pair_groups, query_groups = heads // pair_heads, heads // query_heads
    width = heads * HD
    my_head = lax.axis_index("head")
    me = lax.axis_index("tm")
    scale = 1.0 / math.sqrt(HD)
    slot_of = {slot: i for i, slot in enumerate(slots)}
    order = sending_order(count_head)

    def columns_of(owner, first, count):
        return pl.ds(pl.multiple_of(owner * width + first * HD, HD), count * HD)

    def head_copy(which, offset, g):
        peer = partner(my_head, offset, count_head)
        if which < 2:
            return pltpu.make_async_remote_copy(
                src_ref=(key_ref, value_ref)[which].at[
                    :, :, columns_of(peer, g * pair_heads, pair_heads)
                ],
                dst_ref=pair_in.at[which, g, my_head],
                send_sem=pair_send.at[which, offset - 1, g],
                recv_sem=pair_recv.at[which, offset - 1, g],
                device_id={"head": peer},
                device_id_type=MESH,
            )
        return pltpu.make_async_remote_copy(
            src_ref=query_ref.at[:, :, columns_of(peer, g * query_heads, query_heads)],
            dst_ref=query_in.at[g, my_head],
            send_sem=query_send.at[offset - 1, g],
            recv_sem=query_recv.at[offset - 1, g],
            device_id={"head": peer},
            device_id_type=MESH,
        )

    def local_copy(which, g):
        if which < 2:
            return pltpu.make_async_copy(
                (key_ref, value_ref)[which].at[
                    :, :, columns_of(my_head, g * pair_heads, pair_heads)
                ],
                pair_in.at[which, g, my_head],
                pair_local.at[which, g],
            )
        return pltpu.make_async_copy(
            query_ref.at[:, :, columns_of(my_head, g * query_heads, query_heads)],
            query_in.at[g, my_head],
            query_local.at[g],
        )

    def halo_copy(which, g, slot):
        offset, place = slot
        peer = lax.rem(me + offset, count_tm)
        landing = slot_of[(count_tm - offset, place)]
        return pltpu.make_async_remote_copy(
            src_ref=outbox.at[which, g, slot_of[slot]],
            dst_ref=store.at[which, pl.ds(g * pair_heads, pair_heads), blocks + landing],
            send_sem=halo_send.at[which, g, slot_of[slot]],
            recv_sem=halo_recv.at[which, g, landing],
            device_id={"tm": peer},
            device_id_type=MESH,
        )

    def halo_arrival(which, g, slot):
        i = slot_of[slot]
        peer = lax.rem(me + slot[0], count_tm)
        return pltpu.make_async_remote_copy(
            src_ref=outbox.at[which, g, i],
            dst_ref=store.at[which, pl.ds(g * pair_heads, pair_heads), blocks + i],
            send_sem=halo_send.at[which, g, i],
            recv_sem=halo_recv.at[which, g, i],
            device_id={"tm": peer},
            device_id_type=MESH,
        )

    def beside(slot):
        peer = lax.rem(me + slot[0], count_tm)
        return (peer == me + 1) | (peer == me - 1)

    def if_used(slot, action):
        if slot[1] < FAR_CAP:
            action()
        else:
            pl.when(beside(slot))(action)

    def back_copy(offset, g):
        peer = partner(my_head, offset, count_head)
        return pltpu.make_async_remote_copy(
            src_ref=staged.at[g, peer],
            dst_ref=out_ref.at[:, :, columns_of(my_head, g * query_heads, query_heads)],
            send_sem=back_send.at[offset - 1, g],
            recv_sem=back_recv.at[offset - 1, g],
            device_id={"head": peer},
            device_id_type=MESH,
        )

    def back_own(g):
        return pltpu.make_async_copy(
            staged.at[g, my_head],
            out_ref.at[:, :, columns_of(my_head, g * query_heads, query_heads)],
            back_local.at[g],
        )

    def greet(axis, peer):
        pl.semaphore_signal(
            pltpu.get_barrier_semaphore(), inc=1, device_id={axis: peer}, device_id_type=MESH
        )

    def tell(semaphore, peer):
        pl.semaphore_signal(semaphore, inc=1, device_id={"head": peer}, device_id_type=MESH)

    has_low, has_high = my_head > 0, my_head < count_head - 1
    pl.when(has_low)(lambda: greet("head", my_head - 1))
    pl.when(has_high)(lambda: greet("head", my_head + 1))
    for offset in range(1, count_tm):
        greet("tm", lax.rem(me + offset, count_tm))
    pair_copy = pltpu.make_async_copy(pair_ref, pair_here, pair_sem)
    pair_copy.start()
    tokens_copy = pltpu.make_async_copy(tokens_far, tokens_ref, tokens_sem)
    tokens_copy.start()
    for which, groups in ((0, pair_groups), (1, pair_groups), (2, query_groups)):
        for g in range(groups):
            local_copy(which, g).start()

    def clear(i):
        store[:, :, i] = jnp.zeros((2, heads, block, HD), jnp.bfloat16)

    for i, slot in enumerate(slots):
        if slot[1] >= FAR_CAP:
            pl.when(jnp.logical_not(beside(slot)))(lambda i=i: clear(blocks + i))
    for i in range(blocks + len(slots), padded):
        clear(i)
    sign_ref[...] = sign_table(HD).astype(jnp.bfloat16)

    neighbours = jnp.where(has_low, 1, 0) + jnp.where(has_high, 1, 0)
    pl.semaphore_wait(pltpu.get_barrier_semaphore(), neighbours + count_tm - 1)

    def start_at(distance):
        for offset in order:
            peer = partner(my_head, offset, count_head)
            here = (peer == my_head + distance) | (peer == my_head - distance)
            pl.when(here)(lambda offset=offset: head_copy(0, offset, 0).start())

    for distance in range(1, count_head):
        if distance > 1:
            seen_low, seen_high = my_head >= distance - 1, my_head <= count_head - distance
            low, high = entered_low.at[distance - 2], entered_high.at[distance - 2]
            pl.when(seen_low & has_high)(lambda low=low: tell(low, my_head + 1))
            pl.when(seen_high & has_low)(lambda high=high: tell(high, my_head - 1))
            pl.when(my_head >= distance)(lambda low=low: pl.semaphore_wait(low, 1))
            pl.when(my_head <= count_head - 1 - distance)(
                lambda high=high: pl.semaphore_wait(high, 1)
            )
        start_at(distance)
    for g in range(pair_groups):
        for which in range(2):
            if (which, g) != (0, 0):
                for offset in order:
                    head_copy(which, offset, g).start()
    for g in range(query_groups):
        for offset in order:
            head_copy(2, offset, g).start()

    pair_copy.wait()
    tokens_copy.wait()
    pairs = pair_here[...]
    lane = lax.broadcasted_iota(jnp.int32, (1, LANES), 1)
    listed = jnp.zeros((total_blocks, LANES), jnp.float32)
    token_row = jnp.zeros((1, LANES), jnp.float32)
    for k in range(total_blocks):
        found = jnp.max(jnp.where(pairs == k, 1.0, 0.0), axis=1, keepdims=True)
        here = jnp.where(lane == k, 1.0, 0.0)
        listed = listed + found * here
        token_row = token_row + here * tokens_ref[k].astype(jnp.float32)
    wanted_ref[...] = jnp.zeros_like(wanted_ref)
    for t in range(count_tm):
        of_shard = listed[t * blocks : (t + 1) * blocks]
        listed_ref[t] = of_shard
        wanted_ref[t : t + 1, :] = jnp.max(of_shard, axis=0, keepdims=True)
    low = lax.broadcasted_iota(jnp.int32, (LANES, LANES), 0)
    high = lax.broadcasted_iota(jnp.int32, (LANES, LANES), 1)
    low_shard, high_shard = jnp.zeros_like(low), jnp.zeros_like(high)
    lane_shard = jnp.zeros_like(lane)
    for t in range(1, count_tm):
        low_shard = low_shard + jnp.where(low >= t * blocks, 1, 0)
        high_shard = high_shard + jnp.where(high >= t * blocks, 1, 0)
        lane_shard = lane_shard + jnp.where(lane >= t * blocks, 1, 0)
    before = jnp.where((low_shard == high_shard) & (low < high), 1.0, 0.0).astype(jnp.bfloat16)
    wanted = wanted_ref[...]
    rank = jnp.dot(wanted.astype(jnp.bfloat16), before, preferred_element_type=jnp.float32)
    for place in range(NEAR_CAP):
        chosen = jnp.where(rank == float(place), wanted, 0.0)
        for t in range(count_tm):
            place_ref[place, t] = chosen[t : t + 1, :]
    picks = []
    for offset, place in slots:
        row = place_ref[place, lax.rem(me + offset, count_tm)]
        picks.append(
            [
                jnp.sum(jnp.where(lane == me * blocks + j, row, 0.0), axis=1, keepdims=True)
                for j in range(blocks)
            ]
        )
    mine = listed_ref[me]
    key_lane = lax.broadcasted_iota(jnp.int32, (1, padded * block), 1)
    key_end = jnp.zeros((blocks, padded * block), jnp.float32)
    for i in range(blocks + len(slots)):
        if i < blocks:
            kept_tokens = jnp.where(lane == me * blocks + i, token_row, 0.0)
        else:
            offset, place = slots[i - blocks]
            owner = lax.rem(me + offset, count_tm)
            row = place_ref[place, me]
            kept_tokens = jnp.where(lane_shard == owner, row * token_row, 0.0)
        kept = jnp.sum(mine * kept_tokens, axis=1, keepdims=True)
        inside = jnp.where((key_lane >= i * block) & (key_lane < (i + 1) * block), 1.0, 0.0)
        key_end = key_end + inside * (kept + float(i * block))
    bias_ref[...] = jnp.where(key_lane.astype(jnp.float32) < key_end, 0.0, -1e30)

    def arrived(which, g):
        local_copy(which, g).wait()
        for offset in order:
            head_copy(which, offset, g).wait_recv()

    def rotated(landed, column):
        lanes = pl.ds(pl.multiple_of(column * HD, HD), HD)
        rows = jnp.concatenate(
            [landed[:, b, :, lanes].astype(jnp.float32).reshape(block, HD) for b in range(blocks)],
            axis=0,
        ).astype(jnp.bfloat16)
        turned = jnp.dot(rows, sign_ref[...], preferred_element_type=jnp.float32) * scale
        return turned.astype(jnp.bfloat16)

    def spread(which, g):
        arrived(which, g)

        def one_head(column, carry):
            h = g * pair_heads + column
            turned = rotated(pair_in.at[which, g], column)
            store[which, h, 0:blocks] = turned.reshape(blocks, block, HD)
            wide = turned.astype(jnp.float32)
            for i, slot in enumerate(slots):
                sent = picks[i][0] * wide[0:block]
                for j in range(1, blocks):
                    sent = sent + picks[i][j] * wide[j * block : (j + 1) * block]
                outbox[which, g, i, column] = sent.astype(jnp.bfloat16)
            return carry

        lax.fori_loop(0, pair_heads, one_head, 0)
        for slot in slots:
            if_used(slot, lambda slot=slot: halo_copy(which, g, slot).start())

    position = lax.broadcasted_iota(jnp.int32, (block, HD), 0)

    def attend(g, column):
        h = g * query_heads + column
        query = rotated(query_in.at[g], column)
        keys = store[0, h].reshape(padded * block, HD)
        values = store[1, h].reshape(padded * block, HD)
        scores = lax.dot_general(
            query, keys, (((1,), (1,)), ((), ())), preferred_element_type=jnp.float32
        )
        halves, denominators = [], []
        for b in range(blocks):
            of_block = scores[b * block : (b + 1) * block] * scale + bias_ref[b : b + 1, :]
            peak = jnp.max(of_block, axis=1, keepdims=True)
            weights = jnp.exp(of_block - peak)
            denominators.append(jnp.sum(weights, axis=1, keepdims=True))
            halves.append(weights.astype(jnp.bfloat16))
        mixed = jnp.dot(
            jnp.concatenate(halves, axis=0), values, preferred_element_type=jnp.float32
        )
        mixed = mixed / jnp.concatenate(denominators, axis=0)
        first = mixed.astype(jnp.bfloat16)
        rest = mixed - first.astype(jnp.float32)
        second = rest.astype(jnp.bfloat16)
        third = (rest - second.astype(jnp.float32)).astype(jnp.bfloat16)
        sign = sign_ref[...]
        turned = jnp.dot(
            jnp.concatenate([first, second], axis=1),
            jnp.concatenate([sign, sign], axis=0),
            preferred_element_type=jnp.float32,
        )
        turned = turned + jnp.dot(third, sign, preferred_element_type=jnp.float32)
        turned = turned * scale
        for b in range(blocks):
            live = position < tokens_ref[me * blocks + b]
            result = jnp.where(live, turned[b * block : (b + 1) * block], 0.0)
            for owner in range(count_head):
                staged[g, owner, b, :, column * HD : (column + 1) * HD] = result[
                    owner * part : (owner + 1) * part
                ].astype(jnp.bfloat16)

    def spread_group(g, carry):
        spread(0, g)
        spread(1, g)
        return carry

    lax.fori_loop(0, pair_groups, spread_group, 0)

    def attend_group(g, carry):
        arrived(2, g)

        def halos():
            for which in range(2):
                for slot in slots:
                    if_used(
                        slot,
                        lambda slot=slot, which=which: halo_arrival(
                            which, lax.div(g * query_heads, pair_heads), slot
                        ).wait_recv(),
                    )

        pl.when(lax.rem(g * query_heads, pair_heads) == 0)(halos)
        for column in range(query_heads):
            attend(g, column)
        for offset in order:
            back_copy(offset, g).start()
        back_own(g).start()
        return carry

    lax.fori_loop(0, query_groups, attend_group, 0)

    for g in range(pair_groups):
        for which in range(2):
            for offset in order:
                head_copy(which, offset, g).wait_send()
            for slot in slots:
                if_used(slot, lambda slot=slot, which=which: halo_copy(which, g, slot).wait_send())
    for g in range(query_groups):
        for offset in order:
            head_copy(2, offset, g).wait_send()
            back_copy(offset, g).wait()
        back_own(g).wait()


def shards(query_rows, key_rows, value_rows, pair_list, block_tokens):
    count_head = lax.axis_size("head")
    count_tm = lax.axis_size("tm")
    blocks, part, full_width = query_rows.shape
    block = part * count_head
    heads = full_width // (HD * count_head)
    total_blocks, listed = pair_list.shape
    slots = incoming_slots(count_tm)
    filled = blocks + len(slots)
    per_lane_tile = max(1, LANES // block)
    padded = -(-filled // per_lane_tile) * per_lane_tile
    shard_rows = -(-count_tm // 8) * 8
    pair_heads = heads_together(heads, PAIR_HEADS)
    query_heads = heads_together(pair_heads, QUERY_HEADS)
    pair_groups, query_groups = heads // pair_heads, heads // query_heads
    grouped = (pair_heads, query_heads)
    sizes = (
        count_head, count_tm, blocks, part, heads, block, total_blocks, slots, padded, grouped
    )
    peers = max(1, count_head - 1)
    rounds = max(1, count_head - 2)
    in_hbm = pl.BlockSpec(memory_space=pltpu.HBM)
    dma = pltpu.SemaphoreType.DMA
    return pl.pallas_call(
        functools.partial(kernel, sizes),
        out_shape=jax.ShapeDtypeStruct(query_rows.shape, jnp.bfloat16),
        in_specs=[in_hbm] * 5,
        out_specs=in_hbm,
        scratch_shapes=[
            pltpu.VMEM(
                (2, pair_groups, count_head, blocks, part, pair_heads * HD), jnp.bfloat16
            ),
            pltpu.VMEM((query_groups, count_head, blocks, part, query_heads * HD), jnp.bfloat16),
            pltpu.VMEM((2, heads, padded, block, HD), jnp.bfloat16),
            pltpu.VMEM((2, pair_groups, len(slots), pair_heads, block, HD), jnp.bfloat16),
            pltpu.VMEM((query_groups, count_head, blocks, part, query_heads * HD), jnp.bfloat16),
            pltpu.VMEM((total_blocks, listed), jnp.int32),
            pltpu.SMEM((total_blocks,), jnp.int32),
            pltpu.VMEM((count_tm, blocks, LANES), jnp.float32),
            pltpu.VMEM((NEAR_CAP, count_tm, 1, LANES), jnp.float32),
            pltpu.VMEM((shard_rows, LANES), jnp.float32),
            pltpu.VMEM((blocks, padded * block), jnp.float32),
            pltpu.VMEM((HD, HD), jnp.bfloat16),
            dma((2, peers, pair_groups)),
            dma((2, peers, pair_groups)),
            dma((peers, query_groups)),
            dma((peers, query_groups)),
            dma((2, pair_groups)),
            dma((query_groups,)),
            pltpu.SemaphoreType.REGULAR((rounds,)),
            pltpu.SemaphoreType.REGULAR((rounds,)),
            dma((2, pair_groups, len(slots))),
            dma((2, pair_groups, len(slots))),
            dma((peers, query_groups)),
            dma((peers, query_groups)),
            dma((query_groups,)),
            dma(()),
            dma(()),
        ],
        compiler_params=pltpu.CompilerParams(
            collective_id=0, has_side_effects=True, vmem_limit_bytes=32 * 1024 * 1024
        ),
    )(*[pltpu.with_memory_space_constraint(x, pltpu.HBM) for x in (query_rows, key_rows, value_rows, pair_list, block_tokens)])


def solution(mesh):
    placed = (
        P(("grp", "tm"), "head", None),
        P(("grp", "tm"), "head", None),
        P(("grp", "tm"), "head", None),
        P("grp", None),
        P("grp"),
    )
    return jax.shard_map(
        shards,
        mesh=mesh,
        in_specs=placed,
        out_specs=P(("grp", "tm"), "head", None),
        check_vma=False,
    )
```

```python
import functools
import math

import jax
import jax.numpy as jnp
from jax import lax
from jax.experimental import pallas as pl
from jax.experimental.pallas import tpu as pltpu
from jax.sharding import PartitionSpec as P

HD = 128
NEAR_CAP = 2
FAR_CAP = 1
LANES = 128
EARLY = 2
DEFER = 0
PAIRS_BY_PEER = False
QUERIES_BY_PEER = False
KEY_HEADS = 3
VALUE_HEADS = 3
QUERY_HEADS = 3
MESH = pl.DeviceIdType.MESH


def incoming_slots(count_tm):
    slots = []
    for offset in range(1, count_tm):
        capacity = NEAR_CAP if offset in (1, count_tm - 1) else FAR_CAP
        slots += [(offset, place) for place in range(capacity)]
    return slots


def heads_together(heads, most):
    return max(size for size in range(1, most + 1) if heads % size == 0)


def sign_table(dimension):
    rows = lax.broadcasted_iota(jnp.int32, (dimension, dimension), 0)
    columns = lax.broadcasted_iota(jnp.int32, (dimension, dimension), 1)
    common = rows & columns
    parity = jnp.zeros((dimension, dimension), jnp.int32)
    for bit_level in range(dimension.bit_length() - 1):
        parity = parity + ((common >> bit_level) & 1)
    return jnp.where((parity & 1) == 0, 1.0, -1.0).astype(jnp.float32)


def kernel(
    sizes,
    query_ref,
    key_ref,
    value_ref,
    pair_ref,
    tokens_far,
    out_ref,
    key_in,
    value_in,
    query_in,
    store,
    key_outbox,
    value_outbox,
    key_halo,
    value_halo,
    staged,
    pair_here,
    tokens_ref,
    listed_ref,
    place_ref,
    wanted_ref,
    bias_ref,
    sign_ref,
    head_send,
    head_recv,
    head_local,
    entered_low,
    entered_high,
    column_up,
    column_side,
    column_down,
    halo_send,
    halo_recv,
    back_send,
    back_recv,
    back_local,
    pair_sem,
    tokens_sem,
):
    count_head, count_tm, blocks, part, heads, block, total_blocks, slots, padded, grouped = sizes
    sources, landed = (key_ref, value_ref, query_ref), (key_in, value_in, query_in)
    outbox, halo = (key_outbox, value_outbox), (key_halo, value_halo)
    groups = [heads // size for size in grouped]
    query_heads, query_groups = grouped[2], groups[2]
    offsets = range(1, count_tm)
    places = {o: [p for k, p in slots if k == o] for o in offsets}
    width = heads * HD
    my_head = lax.axis_index("head")
    me = lax.axis_index("tm")
    scale = 1.0 / math.sqrt(HD)
    slot_of = {slot: i for i, slot in enumerate(slots)}
    others = [k + jnp.where(my_head <= k, 1, 0) for k in range(count_head - 1)]
    upper_half = my_head >= count_head // 2
    far_first = [
        jnp.where(upper_half, low, high) for low, high in zip(others, reversed(others))
    ]

    def columns_of(owner, first, count):
        return pl.ds(pl.multiple_of(owner * width + first * HD, HD), count * HD)

    def head_copy(which, peer, g, source=None):
        source = my_head if source is None else source
        return pltpu.make_async_remote_copy(
            src_ref=sources[which].at[:, :, columns_of(peer, g * grouped[which], grouped[which])],
            dst_ref=landed[which].at[g, source],
            send_sem=head_send.at[which, peer, g],
            recv_sem=head_recv.at[which, source, g],
            device_id={"head": peer},
            device_id_type=MESH,
        )

    def local_copy(which, g):
        return pltpu.make_async_copy(
            sources[which].at[:, :, columns_of(my_head, g * grouped[which], grouped[which])],
            landed[which].at[g, my_head],
            head_local.at[which, g],
        )

    def halo_copy(which, g, offset, count, arriving=False):
        peer = lax.rem(me + offset, count_tm)
        first = slot_of[(offset, 0)]
        landing = first if arriving else slot_of[(count_tm - offset, 0)]
        return pltpu.make_async_remote_copy(
            src_ref=outbox[which].at[g, pl.ds(first, count)],
            dst_ref=halo[which].at[g, pl.ds(landing, count)],
            send_sem=halo_send.at[which, g, offset - 1],
            recv_sem=halo_recv.at[which, g, (offset if arriving else count_tm - offset) - 1],
            device_id={"tm": peer},
            device_id_type=MESH,
        )

    def beside(offset):
        peer = lax.rem(me + offset, count_tm)
        return (peer == me + 1) | (peer == me - 1)

    def each_halo(which, g, action, arriving=False):
        for offset in offsets:
            full = len(places[offset])
            if full == FAR_CAP:
                action(halo_copy(which, g, offset, full, arriving))
            else:
                near = beside(offset)
                pl.when(near)(lambda o=offset, n=full: action(halo_copy(which, g, o, n, arriving)))
                pl.when(jnp.logical_not(near))(
                    lambda o=offset: action(halo_copy(which, g, o, FAR_CAP, arriving))
                )

    def back_copy(peer, g, source=None):
        source = my_head if source is None else source
        return pltpu.make_async_remote_copy(
            src_ref=staged.at[g, peer],
            dst_ref=out_ref.at[:, :, columns_of(source, g * query_heads, query_heads)],
            send_sem=back_send.at[peer, g],
            recv_sem=back_recv.at[source, g],
            device_id={"head": peer},
            device_id_type=MESH,
        )

    def back_own(g):
        return pltpu.make_async_copy(
            staged.at[g, my_head],
            out_ref.at[:, :, columns_of(my_head, g * query_heads, query_heads)],
            back_local.at[g],
        )

    def greet(axis, peer):
        pl.semaphore_signal(
            pltpu.get_barrier_semaphore(), inc=1, device_id={axis: peer}, device_id_type=MESH
        )

    def tell(semaphore, peer):
        pl.semaphore_signal(semaphore, inc=1, device_id={"head": peer}, device_id_type=MESH)

    has_low, has_high = my_head > 0, my_head < count_head - 1
    pl.when(has_low)(lambda: greet("head", my_head - 1))
    pl.when(has_high)(lambda: greet("head", my_head + 1))
    hub = my_head == 0

    @pl.when(hub)
    def _():
        for offset in range(1, count_tm):
            greet("tm", lax.rem(me + offset, count_tm))

    pair_copy = pltpu.make_async_copy(pair_ref, pair_here, pair_sem)
    pair_copy.start()
    tokens_copy = pltpu.make_async_copy(tokens_far, tokens_ref, tokens_sem)
    tokens_copy.start()
    for which in range(3):
        for g in range(groups[which]):
            local_copy(which, g).start()

    def clear(i):
        for which in range(2):
            shape = (groups[which], grouped[which], block, HD)
            halo[which][:, i] = jnp.zeros(shape, jnp.bfloat16)

    for i, (offset, place) in enumerate(slots):
        if place >= FAR_CAP:
            pl.when(jnp.logical_not(beside(offset)))(lambda i=i: clear(i))
    sign_ref[...] = sign_table(HD).astype(jnp.bfloat16)

    neighbours = jnp.where(has_low, 1, 0) + jnp.where(has_high, 1, 0)
    awaited = neighbours + jnp.where(hub, count_tm - 1, 0)
    pl.semaphore_wait(pltpu.get_barrier_semaphore(), awaited)

    pairs_of = sorted(
        ((which, g) for which in range(2) for g in range(groups[which])),
        key=lambda piece: piece[1] * grouped[piece[0]],
    )
    queries_of = [(2, g) for g in range(query_groups)]
    early = pairs_of[:EARLY]

    def start_at(distance):
        for side in (-distance, distance):
            peer = my_head + side
            inside = (peer >= 0) & (peer < count_head)
            for which, g in early:
                pl.when(inside)(lambda p=peer, w=which, g=g: head_copy(w, p, g).start())

    for distance in range(1, count_head):
        if distance > 1:
            seen_low, seen_high = my_head >= distance - 1, my_head <= count_head - distance
            low, high = entered_low.at[distance - 2], entered_high.at[distance - 2]
            pl.when(seen_low & has_high)(lambda low=low: tell(low, my_head + 1))
            pl.when(seen_high & has_low)(lambda high=high: tell(high, my_head - 1))
            pl.when(my_head >= distance)(lambda low=low: pl.semaphore_wait(low, 1))
            pl.when(my_head <= count_head - 1 - distance)(
                lambda high=high: pl.semaphore_wait(high, 1)
            )
        start_at(distance)
    pl.when(my_head < count_head - 1)(lambda: pl.semaphore_wait(column_up, 1))
    pl.when(has_low)(lambda: tell(column_up, my_head - 1))

    for pieces, by_peer in ((pairs_of, PAIRS_BY_PEER), (queries_of, QUERIES_BY_PEER)):
        if by_peer:
            plan = [(piece, peer) for peer in far_first for piece in pieces]
        else:
            plan = [(piece, peer) for piece in pieces for peer in far_first]
        for (which, g), peer in plan:
            if (which, g) not in early:
                head_copy(which, peer, g).start()

    @pl.when(hub)
    def _():
        for offset in range(1, count_tm):
            pl.semaphore_signal(
                column_side,
                inc=1,
                device_id={"tm": lax.rem(me + offset, count_tm)},
                device_id_type=MESH,
            )

    pair_copy.wait()
    tokens_copy.wait()
    pairs = pair_here[...]
    lane = lax.broadcasted_iota(jnp.int32, (1, LANES), 1)
    listed = jnp.zeros((total_blocks, LANES), jnp.float32)
    token_row = jnp.zeros((1, LANES), jnp.float32)
    for k in range(total_blocks):
        found = jnp.max(jnp.where(pairs == k, 1.0, 0.0), axis=1, keepdims=True)
        here = jnp.where(lane == k, 1.0, 0.0)
        listed = listed + found * here
        token_row = token_row + here * tokens_ref[k].astype(jnp.float32)
    wanted_ref[...] = jnp.zeros_like(wanted_ref)
    for t in range(count_tm):
        of_shard = listed[t * blocks : (t + 1) * blocks]
        listed_ref[t] = of_shard
        wanted_ref[t : t + 1, :] = jnp.max(of_shard, axis=0, keepdims=True)
    low = lax.broadcasted_iota(jnp.int32, (LANES, LANES), 0)
    high = lax.broadcasted_iota(jnp.int32, (LANES, LANES), 1)
    low_shard, high_shard = jnp.zeros_like(low), jnp.zeros_like(high)
    lane_shard = jnp.zeros_like(lane)
    for t in range(1, count_tm):
        low_shard = low_shard + jnp.where(low >= t * blocks, 1, 0)
        high_shard = high_shard + jnp.where(high >= t * blocks, 1, 0)
        lane_shard = lane_shard + jnp.where(lane >= t * blocks, 1, 0)
    before = jnp.where((low_shard == high_shard) & (low < high), 1.0, 0.0).astype(jnp.bfloat16)
    wanted = wanted_ref[...]
    rank = jnp.dot(wanted.astype(jnp.bfloat16), before, preferred_element_type=jnp.float32)
    for place in range(NEAR_CAP):
        chosen = jnp.where(rank == float(place), wanted, 0.0)
        for t in range(count_tm):
            place_ref[place, t] = chosen[t : t + 1, :]
    picks = []
    for offset, place in slots:
        row = place_ref[place, lax.rem(me + offset, count_tm)]
        picks.append(
            [
                jnp.sum(jnp.where(lane == me * blocks + j, row, 0.0), axis=1, keepdims=True)
                for j in range(blocks)
            ]
        )
    mine = listed_ref[me]
    key_lane = lax.broadcasted_iota(jnp.int32, (1, padded * block), 1)
    key_end = jnp.zeros((blocks, padded * block), jnp.float32)
    for i in range(blocks + len(slots)):
        if i < blocks:
            kept_tokens = jnp.where(lane == me * blocks + i, token_row, 0.0)
        else:
            offset, place = slots[i - blocks]
            owner = lax.rem(me + offset, count_tm)
            row = place_ref[place, me]
            kept_tokens = jnp.where(lane_shard == owner, row * token_row, 0.0)
        kept = jnp.sum(mine * kept_tokens, axis=1, keepdims=True)
        inside = jnp.where((key_lane >= i * block) & (key_lane < (i + 1) * block), 1.0, 0.0)
        key_end = key_end + inside * (kept + float(i * block))
    bias_ref[...] = jnp.where(key_lane.astype(jnp.float32) < key_end, 0.0, -1e30)

    def arrived(which, g):
        local_copy(which, g).wait()
        for peer in others:
            head_copy(which, peer, g, source=peer).wait_recv()

    def rotated(which, g, column):
        lanes = pl.ds(pl.multiple_of(column * HD, HD), HD)
        rows = jnp.concatenate(
            [
                landed[which][g, :, b, :, lanes].astype(jnp.float32).reshape(block, HD)
                for b in range(blocks)
            ],
            axis=0,
        ).astype(jnp.bfloat16)
        turned = jnp.dot(rows, sign_ref[...], preferred_element_type=jnp.float32) * scale
        return turned.astype(jnp.bfloat16)

    def spread(which, g):
        arrived(which, g)

        def one_head(column, carry):
            turned = rotated(which, g, column)
            store[which, g * grouped[which] + column] = turned
            wide = turned.astype(jnp.float32)
            for i in range(len(slots)):
                sent = picks[i][0] * wide[0:block]
                for j in range(1, blocks):
                    sent = sent + picks[i][j] * wide[j * block : (j + 1) * block]
                outbox[which][g, i, column] = sent.astype(jnp.bfloat16)
            return carry

        lax.fori_loop(0, grouped[which], one_head, 0)
        each_halo(which, g, lambda copy: copy.start())

    position = lax.broadcasted_iota(jnp.int32, (block, HD), 0)
    spare = padded - blocks - len(slots)

    to_base_two = scale * math.log2(math.e)

    def listed_rows(which, h):
        pieces = [store[which, h]]
        for i in range(len(slots)):
            pieces.append(halo[which][lax.div(h, grouped[which]), i, lax.rem(h, grouped[which])])
        if spare > 0:
            pieces.append(jnp.zeros((spare * block, HD), jnp.bfloat16))
        return jnp.concatenate(pieces, axis=0)

    def softmax(scores):
        halves, denominators = [], []
        for b in range(blocks):
            of_block = scores[b * block : (b + 1) * block] + bias_ref[b : b + 1, :]
            peak = jnp.max(of_block, axis=1, keepdims=True)
            weights = jnp.exp2((of_block - peak) * to_base_two)
            denominators.append(jnp.sum(weights, axis=1, keepdims=True))
            halves.append(weights.astype(jnp.bfloat16))
        return jnp.concatenate(halves, axis=0), 1.0 / jnp.concatenate(denominators, axis=0)

    def turned_back(mixed):
        first = mixed.astype(jnp.bfloat16)
        rest = mixed - first.astype(jnp.float32)
        second = rest.astype(jnp.bfloat16)
        third = (rest - second.astype(jnp.float32)).astype(jnp.bfloat16)
        sign = sign_ref[...]
        turned = jnp.dot(
            jnp.concatenate([first, second], axis=1),
            jnp.concatenate([sign, sign], axis=0),
            preferred_element_type=jnp.float32,
        )
        return (turned + jnp.dot(third, sign, preferred_element_type=jnp.float32)) * scale

    def attend(g):
        columns = range(query_heads)
        queries = [rotated(2, g, column) for column in columns]
        scores = [
            lax.dot_general(
                queries[column],
                listed_rows(0, g * query_heads + column),
                (((1,), (1,)), ((), ())),
                preferred_element_type=jnp.float32,
            )
            for column in columns
        ]
        weighted = [softmax(of_head) for of_head in scores]
        mixed = [
            jnp.dot(
                weighted[column][0],
                listed_rows(1, g * query_heads + column),
                preferred_element_type=jnp.float32,
            )
            * weighted[column][1]
            for column in columns
        ]
        results = [turned_back(of_head) for of_head in mixed]
        for b in range(blocks):
            live = position < tokens_ref[me * blocks + b]
            for column in columns:
                result = jnp.where(live, results[column][b * block : (b + 1) * block], 0.0)
                for owner in range(count_head):
                    staged[g, owner, b, :, column * HD : (column + 1) * HD] = result[
                        owner * part : (owner + 1) * part
                    ].astype(jnp.bfloat16)

    pl.when(hub)(lambda: pl.semaphore_wait(column_side, count_tm - 1))
    pl.when(has_low)(lambda: pl.semaphore_wait(column_down, 1))
    pl.when(has_high)(lambda: tell(column_down, my_head + 1))
    for which, g in pairs_of:
        spread(which, g)

    def attend_group(g, carry):
        arrived(2, g)
        for which in range(2):
            for j in range(groups[which]):
                first = j * grouped[which] - g * query_heads
                pl.when((first >= 0) & (first < query_heads))(
                    lambda which=which, j=j: each_halo(
                        which, j, lambda copy: copy.wait_recv(), arriving=True
                    )
                )
        attend(g)
        for peer in far_first:
            pl.when(first_served(peer))(lambda peer=peer: back_copy(peer, g).start())
        back_own(g).start()
        pl.when(g >= DEFER)(lambda: send_later(g - DEFER))
        return carry

    def first_served(peer):
        return (my_head == 0) | (peer == 0)

    def send_later(g):
        for peer in far_first:
            later = jnp.logical_not(first_served(peer))
            pl.when(later)(lambda peer=peer: back_copy(peer, g).start())

    lax.fori_loop(0, query_groups, attend_group, 0)
    for g in range(max(0, query_groups - DEFER), query_groups):
        send_later(g)

    for which in range(3):
        for g in range(groups[which]):
            for peer in others:
                head_copy(which, peer, g).wait_send()
            if which < 2:
                each_halo(which, g, lambda copy: copy.wait_send())
    for g in range(query_groups):
        for peer in others:
            back_copy(peer, g).wait_send()
            back_copy(peer, g, source=peer).wait_recv()
        back_own(g).wait()


def shards(query_rows, key_rows, value_rows, pair_list, block_tokens):
    count_head = lax.axis_size("head")
    count_tm = lax.axis_size("tm")
    blocks, part, full_width = query_rows.shape
    block = part * count_head
    heads = full_width // (HD * count_head)
    total_blocks, listed = pair_list.shape
    slots = incoming_slots(count_tm)
    filled = blocks + len(slots)
    per_lane_tile = max(1, LANES // block)
    padded = -(-filled // per_lane_tile) * per_lane_tile
    shard_rows = -(-count_tm // 8) * 8
    key_heads = heads_together(heads, KEY_HEADS)
    value_heads = heads_together(heads, VALUE_HEADS)
    query_heads = heads_together(heads, QUERY_HEADS)
    grouped = (key_heads, value_heads, query_heads)
    key_groups, value_groups, query_groups = [heads // size for size in grouped]
    most = max(key_groups, value_groups, query_groups)
    sizes = (
        count_head, count_tm, blocks, part, heads, block, total_blocks, slots, padded, grouped
    )
    rounds = max(1, count_head - 2)
    in_hbm = pl.BlockSpec(memory_space=pltpu.HBM)
    dma = pltpu.SemaphoreType.DMA
    return pl.pallas_call(
        functools.partial(kernel, sizes),
        out_shape=jax.ShapeDtypeStruct(query_rows.shape, jnp.bfloat16),
        in_specs=[in_hbm] * 5,
        out_specs=in_hbm,
        scratch_shapes=[
            pltpu.VMEM((key_groups, count_head, blocks, part, key_heads * HD), jnp.bfloat16),
            pltpu.VMEM((value_groups, count_head, blocks, part, value_heads * HD), jnp.bfloat16),
            pltpu.VMEM((query_groups, count_head, blocks, part, query_heads * HD), jnp.bfloat16),
            pltpu.VMEM((2, heads, blocks * block, HD), jnp.bfloat16),
            pltpu.VMEM((key_groups, len(slots), key_heads, block, HD), jnp.bfloat16),
            pltpu.VMEM((value_groups, len(slots), value_heads, block, HD), jnp.bfloat16),
            pltpu.VMEM((key_groups, len(slots), key_heads, block, HD), jnp.bfloat16),
            pltpu.VMEM((value_groups, len(slots), value_heads, block, HD), jnp.bfloat16),
            pltpu.VMEM((query_groups, count_head, blocks, part, query_heads * HD), jnp.bfloat16),
            pltpu.VMEM((total_blocks, listed), jnp.int32),
            pltpu.SMEM((total_blocks,), jnp.int32),
            pltpu.VMEM((count_tm, blocks, LANES), jnp.float32),
            pltpu.VMEM((NEAR_CAP, count_tm, 1, LANES), jnp.float32),
            pltpu.VMEM((shard_rows, LANES), jnp.float32),
            pltpu.VMEM((blocks, padded * block), jnp.float32),
            pltpu.VMEM((HD, HD), jnp.bfloat16),
            dma((3, count_head, most)),
            dma((3, count_head, most)),
            dma((3, most)),
            pltpu.SemaphoreType.REGULAR((rounds,)),
            pltpu.SemaphoreType.REGULAR((rounds,)),
            pltpu.SemaphoreType.REGULAR,
            pltpu.SemaphoreType.REGULAR,
            pltpu.SemaphoreType.REGULAR,
            dma((2, most, count_tm - 1)),
            dma((2, most, count_tm - 1)),
            dma((count_head, query_groups)),
            dma((count_head, query_groups)),
            dma((query_groups,)),
            dma(()),
            dma(()),
        ],
        compiler_params=pltpu.CompilerParams(
            collective_id=0, has_side_effects=True, vmem_limit_bytes=32 * 1024 * 1024
        ),
    )(*[pltpu.with_memory_space_constraint(x, pltpu.HBM) for x in (query_rows, key_rows, value_rows, pair_list, block_tokens)])


def solution(mesh):
    placed = (
        P(("grp", "tm"), "head", None),
        P(("grp", "tm"), "head", None),
        P(("grp", "tm"), "head", None),
        P("grp", None),
        P("grp"),
    )
    return jax.shard_map(
        shards,
        mesh=mesh,
        in_specs=placed,
        out_specs=P(("grp", "tm"), "head", None),
        check_vma=False,
    )
```

```python
import functools
import math

import jax
import jax.numpy as jnp
from jax import lax
from jax.experimental import pallas as pl
from jax.experimental.pallas import tpu as pltpu
from jax.sharding import PartitionSpec as P

HD = 128
NEAR_CAP = 2
FAR_CAP = 1
LANES = 128
EARLY = 2
DEFER = 1
PAIR_HEADS = 2
QUERY_HEADS = 2
MESH = pl.DeviceIdType.MESH


def incoming_slots(count_tm):
    slots = []
    for offset in range(1, count_tm):
        capacity = NEAR_CAP if offset in (1, count_tm - 1) else FAR_CAP
        slots += [(offset, place) for place in range(capacity)]
    return slots


def heads_together(heads, most):
    return max(size for size in range(1, most + 1) if heads % size == 0)


def sign_table(dimension):
    rows = lax.broadcasted_iota(jnp.int32, (dimension, dimension), 0)
    columns = lax.broadcasted_iota(jnp.int32, (dimension, dimension), 1)
    common = rows & columns
    parity = jnp.zeros((dimension, dimension), jnp.int32)
    for bit_level in range(dimension.bit_length() - 1):
        parity = parity + ((common >> bit_level) & 1)
    return jnp.where((parity & 1) == 0, 1.0, -1.0).astype(jnp.float32)


def kernel(
    sizes,
    query_ref,
    key_ref,
    value_ref,
    pair_ref,
    tokens_far,
    out_ref,
    packed,
    pair_in,
    query_in,
    store,
    outbox,
    halo,
    staged,
    pair_here,
    tokens_ref,
    listed_ref,
    place_ref,
    wanted_ref,
    bias_ref,
    sign_ref,
    head_send,
    head_recv,
    pair_local,
    query_local,
    pack_sem,
    entered_low,
    entered_high,
    column_up,
    column_side,
    column_down,
    halo_send,
    halo_recv,
    back_send,
    back_recv,
    back_local,
    pair_sem,
    tokens_sem,
):
    count_head, count_tm, blocks, part, heads, block, total_blocks, slots, padded, grouped = sizes
    pairs = (key_ref, value_ref)
    pair_heads, query_heads = grouped
    pair_groups, query_groups = heads // pair_heads, heads // query_heads
    offsets = range(1, count_tm)
    places = {o: [p for k, p in slots if k == o] for o in offsets}
    width = heads * HD
    my_head = lax.axis_index("head")
    me = lax.axis_index("tm")
    scale = 1.0 / math.sqrt(HD)
    slot_of = {slot: i for i, slot in enumerate(slots)}
    others = [k + jnp.where(my_head <= k, 1, 0) for k in range(count_head - 1)]
    upper_half = my_head >= count_head // 2
    far_first = [
        jnp.where(upper_half, low, high) for low, high in zip(others, reversed(others))
    ]

    def columns_of(owner, first, count):
        return pl.ds(pl.multiple_of(owner * width + first * HD, HD), count * HD)

    def head_copy(is_query, peer, g, source=None):
        source = my_head if source is None else source
        if is_query:
            sent = query_ref.at[:, :, columns_of(peer, g * query_heads, query_heads)]
            landing = query_in.at[g, source]
        else:
            sent, landing = packed.at[g, peer], pair_in.at[g, source]
        return pltpu.make_async_remote_copy(
            src_ref=sent,
            dst_ref=landing,
            send_sem=head_send.at[is_query, peer, g],
            recv_sem=head_recv.at[is_query, source, g],
            device_id={"head": peer},
            device_id_type=MESH,
        )

    def pair_columns(which, owner, g):
        return pairs[which].at[:, :, columns_of(owner, g * pair_heads, pair_heads)]

    def pack_copy(which, peer, g):
        return pltpu.make_async_copy(
            pair_columns(which, peer, g), packed.at[g, peer, which], pack_sem.at[which, peer, g]
        )

    def own_pair(which, g):
        return pltpu.make_async_copy(
            pair_columns(which, my_head, g),
            pair_in.at[g, my_head, which],
            pair_local.at[which, g],
        )

    def own_query(g):
        return pltpu.make_async_copy(
            query_ref.at[:, :, columns_of(my_head, g * query_heads, query_heads)],
            query_in.at[g, my_head],
            query_local.at[g],
        )

    def halo_copy(g, offset, count, arriving=False):
        peer = lax.rem(me + offset, count_tm)
        first = slot_of[(offset, 0)]
        landing = first if arriving else slot_of[(count_tm - offset, 0)]
        return pltpu.make_async_remote_copy(
            src_ref=outbox.at[g, pl.ds(first, count)],
            dst_ref=halo.at[g, pl.ds(landing, count)],
            send_sem=halo_send.at[g, offset - 1],
            recv_sem=halo_recv.at[g, (offset if arriving else count_tm - offset) - 1],
            device_id={"tm": peer},
            device_id_type=MESH,
        )

    def beside(offset):
        peer = lax.rem(me + offset, count_tm)
        return (peer == me + 1) | (peer == me - 1)

    def each_halo(g, action, arriving=False):
        for offset in offsets:
            full = len(places[offset])
            if full == FAR_CAP:
                action(halo_copy(g, offset, full, arriving))
            else:
                near = beside(offset)
                pl.when(near)(lambda o=offset, n=full: action(halo_copy(g, o, n, arriving)))
                pl.when(jnp.logical_not(near))(
                    lambda o=offset: action(halo_copy(g, o, FAR_CAP, arriving))
                )

    def back_copy(peer, g, source=None):
        source = my_head if source is None else source
        return pltpu.make_async_remote_copy(
            src_ref=staged.at[g, peer],
            dst_ref=out_ref.at[:, :, columns_of(source, g * query_heads, query_heads)],
            send_sem=back_send.at[peer, g],
            recv_sem=back_recv.at[source, g],
            device_id={"head": peer},
            device_id_type=MESH,
        )

    def back_own(g):
        return pltpu.make_async_copy(
            staged.at[g, my_head],
            out_ref.at[:, :, columns_of(my_head, g * query_heads, query_heads)],
            back_local.at[g],
        )

    def greet(axis, peer):
        pl.semaphore_signal(
            pltpu.get_barrier_semaphore(), inc=1, device_id={axis: peer}, device_id_type=MESH
        )

    def tell(semaphore, peer):
        pl.semaphore_signal(semaphore, inc=1, device_id={"head": peer}, device_id_type=MESH)

    has_low, has_high = my_head > 0, my_head < count_head - 1
    pl.when(has_low)(lambda: greet("head", my_head - 1))
    pl.when(has_high)(lambda: greet("head", my_head + 1))
    hub = my_head == 0

    @pl.when(hub)
    def _():
        for offset in range(1, count_tm):
            greet("tm", lax.rem(me + offset, count_tm))

    pair_copy = pltpu.make_async_copy(pair_ref, pair_here, pair_sem)
    pair_copy.start()
    tokens_copy = pltpu.make_async_copy(tokens_far, tokens_ref, tokens_sem)
    tokens_copy.start()
    for g in range(pair_groups):
        for peer in others:
            for which in range(2):
                pack_copy(which, peer, g).start()
        for which in range(2):
            own_pair(which, g).start()
    for g in range(query_groups):
        own_query(g).start()

    def clear(i):
        halo[:, i] = jnp.zeros((pair_groups, 2, pair_heads, block, HD), jnp.bfloat16)

    for i, (offset, place) in enumerate(slots):
        if place >= FAR_CAP:
            pl.when(jnp.logical_not(beside(offset)))(lambda i=i: clear(i))
    sign_ref[...] = sign_table(HD).astype(jnp.bfloat16)

    neighbours = jnp.where(has_low, 1, 0) + jnp.where(has_high, 1, 0)
    awaited = neighbours + jnp.where(hub, count_tm - 1, 0)
    pl.semaphore_wait(pltpu.get_barrier_semaphore(), awaited)

    pieces = [(0, g) for g in range(pair_groups)] + [(1, g) for g in range(query_groups)]
    early = pieces[: min(EARLY, pair_groups)]
    for _, g in early:
        for peer in others:
            for which in range(2):
                pack_copy(which, peer, g).wait()

    def start_at(distance):
        for side in (-distance, distance):
            peer = my_head + side
            inside = (peer >= 0) & (peer < count_head)
            for kind, g in early:
                pl.when(inside)(lambda p=peer, k=kind, g=g: head_copy(k, p, g).start())

    for distance in range(1, count_head):
        if distance > 1:
            seen_low, seen_high = my_head >= distance - 1, my_head <= count_head - distance
            low, high = entered_low.at[distance - 2], entered_high.at[distance - 2]
            pl.when(seen_low & has_high)(lambda low=low: tell(low, my_head + 1))
            pl.when(seen_high & has_low)(lambda high=high: tell(high, my_head - 1))
            pl.when(my_head >= distance)(lambda low=low: pl.semaphore_wait(low, 1))
            pl.when(my_head <= count_head - 1 - distance)(
                lambda high=high: pl.semaphore_wait(high, 1)
            )
        start_at(distance)
    pl.when(my_head < count_head - 1)(lambda: pl.semaphore_wait(column_up, 1))
    pl.when(has_low)(lambda: tell(column_up, my_head - 1))

    for kind, g in pieces:
        if (kind, g) not in early:
            for peer in far_first:
                if kind == 0:
                    for which in range(2):
                        pack_copy(which, peer, g).wait()
                head_copy(kind, peer, g).start()

    @pl.when(hub)
    def _():
        for offset in range(1, count_tm):
            pl.semaphore_signal(
                column_side,
                inc=1,
                device_id={"tm": lax.rem(me + offset, count_tm)},
                device_id_type=MESH,
            )

    pair_copy.wait()
    tokens_copy.wait()
    listing = pair_here[...]
    lane = lax.broadcasted_iota(jnp.int32, (1, LANES), 1)
    listed = jnp.zeros((total_blocks, LANES), jnp.float32)
    token_row = jnp.zeros((1, LANES), jnp.float32)
    for k in range(total_blocks):
        found = jnp.max(jnp.where(listing == k, 1.0, 0.0), axis=1, keepdims=True)
        here = jnp.where(lane == k, 1.0, 0.0)
        listed = listed + found * here
        token_row = token_row + here * tokens_ref[k].astype(jnp.float32)
    wanted_ref[...] = jnp.zeros_like(wanted_ref)
    for t in range(count_tm):
        of_shard = listed[t * blocks : (t + 1) * blocks]
        listed_ref[t] = of_shard
        wanted_ref[t : t + 1, :] = jnp.max(of_shard, axis=0, keepdims=True)
    low = lax.broadcasted_iota(jnp.int32, (LANES, LANES), 0)
    high = lax.broadcasted_iota(jnp.int32, (LANES, LANES), 1)
    low_shard, high_shard = jnp.zeros_like(low), jnp.zeros_like(high)
    lane_shard = jnp.zeros_like(lane)
    for t in range(1, count_tm):
        low_shard = low_shard + jnp.where(low >= t * blocks, 1, 0)
        high_shard = high_shard + jnp.where(high >= t * blocks, 1, 0)
        lane_shard = lane_shard + jnp.where(lane >= t * blocks, 1, 0)
    before = jnp.where((low_shard == high_shard) & (low < high), 1.0, 0.0).astype(jnp.bfloat16)
    wanted = wanted_ref[...]
    rank = jnp.dot(wanted.astype(jnp.bfloat16), before, preferred_element_type=jnp.float32)
    for place in range(NEAR_CAP):
        chosen = jnp.where(rank == float(place), wanted, 0.0)
        for t in range(count_tm):
            place_ref[place, t] = chosen[t : t + 1, :]
    picks = []
    for offset, place in slots:
        row = place_ref[place, lax.rem(me + offset, count_tm)]
        picks.append(
            [
                jnp.sum(jnp.where(lane == me * blocks + j, row, 0.0), axis=1, keepdims=True)
                for j in range(blocks)
            ]
        )
    mine = listed_ref[me]
    key_lane = lax.broadcasted_iota(jnp.int32, (1, padded * block), 1)
    key_end = jnp.zeros((blocks, padded * block), jnp.float32)
    for i in range(blocks + len(slots)):
        if i < blocks:
            kept_tokens = jnp.where(lane == me * blocks + i, token_row, 0.0)
        else:
            offset, place = slots[i - blocks]
            owner = lax.rem(me + offset, count_tm)
            row = place_ref[place, me]
            kept_tokens = jnp.where(lane_shard == owner, row * token_row, 0.0)
        kept = jnp.sum(mine * kept_tokens, axis=1, keepdims=True)
        inside = jnp.where((key_lane >= i * block) & (key_lane < (i + 1) * block), 1.0, 0.0)
        key_end = key_end + inside * (kept + float(i * block))
    bias_ref[...] = jnp.where(key_lane.astype(jnp.float32) < key_end, 0.0, -1e30)

    def arrived(kind, g):
        for peer in others:
            head_copy(kind, peer, g, source=peer).wait_recv()

    def rotated(landed, column):
        lanes = pl.ds(pl.multiple_of(column * HD, HD), HD)
        rows = jnp.concatenate(
            [landed[:, b, :, lanes].astype(jnp.float32).reshape(block, HD) for b in range(blocks)],
            axis=0,
        ).astype(jnp.bfloat16)
        turned = jnp.dot(rows, sign_ref[...], preferred_element_type=jnp.float32) * scale
        return turned.astype(jnp.bfloat16)

    def spread(g, carry):
        for which in range(2):
            own_pair(which, g).wait()
        arrived(0, g)

        def one_head(column, carry):
            for which in range(2):
                turned = rotated(pair_in.at[g, :, which], column)
                store[which, g * pair_heads + column] = turned
                wide = turned.astype(jnp.float32)
                for i in range(len(slots)):
                    sent = picks[i][0] * wide[0:block]
                    for j in range(1, blocks):
                        sent = sent + picks[i][j] * wide[j * block : (j + 1) * block]
                    outbox[g, i, which, column] = sent.astype(jnp.bfloat16)
            return carry

        lax.fori_loop(0, pair_heads, one_head, 0)
        each_halo(g, lambda copy: copy.start())
        return carry

    position = lax.broadcasted_iota(jnp.int32, (block, HD), 0)
    spare = padded - blocks - len(slots)

    to_base_two = scale * math.log2(math.e)

    def listed_rows(which, h):
        pieces = [store[which, h]]
        for i in range(len(slots)):
            pieces.append(halo[lax.div(h, pair_heads), i, which, lax.rem(h, pair_heads)])
        if spare > 0:
            pieces.append(jnp.zeros((spare * block, HD), jnp.bfloat16))
        return jnp.concatenate(pieces, axis=0)

    def softmax(scores):
        halves, denominators = [], []
        for b in range(blocks):
            of_block = scores[b * block : (b + 1) * block] + bias_ref[b : b + 1, :]
            peak = jnp.max(of_block, axis=1, keepdims=True)
            weights = jnp.exp2((of_block - peak) * to_base_two)
            denominators.append(jnp.sum(weights, axis=1, keepdims=True))
            halves.append(weights.astype(jnp.bfloat16))
        return jnp.concatenate(halves, axis=0), 1.0 / jnp.concatenate(denominators, axis=0)

    def turned_back(mixed):
        first = mixed.astype(jnp.bfloat16)
        rest = mixed - first.astype(jnp.float32)
        second = rest.astype(jnp.bfloat16)
        third = (rest - second.astype(jnp.float32)).astype(jnp.bfloat16)
        sign = sign_ref[...]
        turned = jnp.dot(
            jnp.concatenate([first, second], axis=1),
            jnp.concatenate([sign, sign], axis=0),
            preferred_element_type=jnp.float32,
        )
        return (turned + jnp.dot(third, sign, preferred_element_type=jnp.float32)) * scale

    def attend(g):
        columns = range(query_heads)
        queries = [rotated(query_in.at[g], column) for column in columns]
        scores = [
            lax.dot_general(
                queries[column],
                listed_rows(0, g * query_heads + column),
                (((1,), (1,)), ((), ())),
                preferred_element_type=jnp.float32,
            )
            for column in columns
        ]
        weighted = [softmax(of_head) for of_head in scores]
        mixed = [
            jnp.dot(
                weighted[column][0],
                listed_rows(1, g * query_heads + column),
                preferred_element_type=jnp.float32,
            )
            * weighted[column][1]
            for column in columns
        ]
        results = [turned_back(of_head) for of_head in mixed]
        for b in range(blocks):
            live = position < tokens_ref[me * blocks + b]
            for column in columns:
                result = jnp.where(live, results[column][b * block : (b + 1) * block], 0.0)
                for owner in range(count_head):
                    staged[g, owner, b, :, column * HD : (column + 1) * HD] = result[
                        owner * part : (owner + 1) * part
                    ].astype(jnp.bfloat16)

    pl.when(hub)(lambda: pl.semaphore_wait(column_side, count_tm - 1))
    pl.when(has_low)(lambda: pl.semaphore_wait(column_down, 1))
    pl.when(has_high)(lambda: tell(column_down, my_head + 1))
    lax.fori_loop(0, pair_groups, spread, 0)

    def attend_group(g, carry):
        own_query(g).wait()
        arrived(1, g)
        for j in range(pair_groups):
            first = j * pair_heads - g * query_heads
            pl.when((first >= 0) & (first < query_heads))(
                lambda j=j: each_halo(j, lambda copy: copy.wait_recv(), arriving=True)
            )
        attend(g)
        for peer in far_first:
            now = jnp.logical_not(deferred(peer))
            pl.when(now)(lambda peer=peer: back_copy(peer, g).start())
        back_own(g).start()
        pl.when(g >= DEFER)(lambda: send_deferred(g - DEFER))
        return carry

    def deferred(peer):
        return (my_head > 0) & (peer > 0)

    def send_deferred(g):
        for peer in far_first:
            pl.when(deferred(peer))(lambda peer=peer: back_copy(peer, g).start())

    lax.fori_loop(0, query_groups, attend_group, 0)
    for g in range(max(0, query_groups - DEFER), query_groups):
        send_deferred(g)

    for kind, g in pieces:
        for peer in others:
            head_copy(kind, peer, g).wait_send()
        if kind == 0:
            each_halo(g, lambda copy: copy.wait_send())
    for g in range(query_groups):
        for peer in others:
            back_copy(peer, g).wait_send()
            back_copy(peer, g, source=peer).wait_recv()
        back_own(g).wait()


def shards(query_rows, key_rows, value_rows, pair_list, block_tokens):
    count_head = lax.axis_size("head")
    count_tm = lax.axis_size("tm")
    blocks, part, full_width = query_rows.shape
    block = part * count_head
    heads = full_width // (HD * count_head)
    total_blocks, listed = pair_list.shape
    slots = incoming_slots(count_tm)
    filled = blocks + len(slots)
    per_lane_tile = max(1, LANES // block)
    padded = -(-filled // per_lane_tile) * per_lane_tile
    shard_rows = -(-count_tm // 8) * 8
    pair_heads = heads_together(heads, PAIR_HEADS)
    query_heads = heads_together(heads, QUERY_HEADS)
    grouped = (pair_heads, query_heads)
    pair_groups, query_groups = [heads // size for size in grouped]
    most = max(pair_groups, query_groups)
    pair_shape = (pair_groups, count_head, 2, blocks, part, pair_heads * HD)
    query_shape = (query_groups, count_head, blocks, part, query_heads * HD)
    halo_shape = (pair_groups, len(slots), 2, pair_heads, block, HD)
    sizes = (
        count_head, count_tm, blocks, part, heads, block, total_blocks, slots, padded, grouped
    )
    rounds = max(1, count_head - 2)
    in_hbm = pl.BlockSpec(memory_space=pltpu.HBM)
    dma = pltpu.SemaphoreType.DMA
    return pl.pallas_call(
        functools.partial(kernel, sizes),
        out_shape=jax.ShapeDtypeStruct(query_rows.shape, jnp.bfloat16),
        in_specs=[in_hbm] * 5,
        out_specs=in_hbm,
        scratch_shapes=[
            pltpu.VMEM(pair_shape, jnp.bfloat16),
            pltpu.VMEM(pair_shape, jnp.bfloat16),
            pltpu.VMEM(query_shape, jnp.bfloat16),
            pltpu.VMEM((2, heads, blocks * block, HD), jnp.bfloat16),
            pltpu.VMEM(halo_shape, jnp.bfloat16),
            pltpu.VMEM(halo_shape, jnp.bfloat16),
            pltpu.VMEM(query_shape, jnp.bfloat16),
            pltpu.VMEM((total_blocks, listed), jnp.int32),
            pltpu.SMEM((total_blocks,), jnp.int32),
            pltpu.VMEM((count_tm, blocks, LANES), jnp.float32),
            pltpu.VMEM((NEAR_CAP, count_tm, 1, LANES), jnp.float32),
            pltpu.VMEM((shard_rows, LANES), jnp.float32),
            pltpu.VMEM((blocks, padded * block), jnp.float32),
            pltpu.VMEM((HD, HD), jnp.bfloat16),
            dma((2, count_head, most)),
            dma((2, count_head, most)),
            dma((2, pair_groups)),
            dma((query_groups,)),
            dma((2, count_head, pair_groups)),
            pltpu.SemaphoreType.REGULAR((rounds,)),
            pltpu.SemaphoreType.REGULAR((rounds,)),
            pltpu.SemaphoreType.REGULAR,
            pltpu.SemaphoreType.REGULAR,
            pltpu.SemaphoreType.REGULAR,
            dma((pair_groups, count_tm - 1)),
            dma((pair_groups, count_tm - 1)),
            dma((count_head, query_groups)),
            dma((count_head, query_groups)),
            dma((query_groups,)),
            dma(()),
            dma(()),
        ],
        compiler_params=pltpu.CompilerParams(
            collective_id=0, has_side_effects=True, vmem_limit_bytes=32 * 1024 * 1024
        ),
    )(*[pltpu.with_memory_space_constraint(x, pltpu.HBM) for x in (query_rows, key_rows, value_rows, pair_list, block_tokens)])


def solution(mesh):
    placed = (
        P(("grp", "tm"), "head", None),
        P(("grp", "tm"), "head", None),
        P(("grp", "tm"), "head", None),
        P("grp", None),
        P("grp"),
    )
    return jax.shard_map(
        shards,
        mesh=mesh,
        in_specs=placed,
        out_specs=P(("grp", "tm"), "head", None),
        check_vma=False,
    )
```

```python
import functools
import math

import jax
import jax.numpy as jnp
from jax import lax
from jax.experimental import pallas as pl
from jax.experimental.pallas import tpu as pltpu
from jax.sharding import PartitionSpec as P

HD = 128
NEAR_CAP = 2
FAR_CAP = 1
LANES = 128
EARLY = 2
DEFER = 1
PAIR_HEADS = 2
QUERY_HEADS = 2
MESH = pl.DeviceIdType.MESH


def incoming_slots(count_tm):
    slots = []
    for offset in range(1, count_tm):
        capacity = NEAR_CAP if offset in (1, count_tm - 1) else FAR_CAP
        slots += [(offset, place) for place in range(capacity)]
    return slots


def heads_together(heads, most):
    return max(size for size in range(1, most + 1) if heads % size == 0)


def sign_table(dimension):
    rows = lax.broadcasted_iota(jnp.int32, (dimension, dimension), 0)
    columns = lax.broadcasted_iota(jnp.int32, (dimension, dimension), 1)
    common = rows & columns
    parity = jnp.zeros((dimension, dimension), jnp.int32)
    for bit_level in range(dimension.bit_length() - 1):
        parity = parity + ((common >> bit_level) & 1)
    return jnp.where((parity & 1) == 0, 1.0, -1.0).astype(jnp.float32)


def kernel(
    sizes,
    query_ref,
    key_ref,
    value_ref,
    pair_ref,
    tokens_far,
    out_ref,
    packed,
    pair_in,
    query_in,
    store,
    outbox,
    halo,
    staged,
    pair_here,
    tokens_ref,
    listed_ref,
    place_ref,
    wanted_ref,
    bias_ref,
    sign_ref,
    head_send,
    head_recv,
    pair_local,
    query_local,
    pack_sem,
    entered_low,
    entered_high,
    column_up,
    column_side,
    column_down,
    halo_send,
    halo_recv,
    back_send,
    back_recv,
    back_local,
    pair_sem,
    tokens_sem,
):
    count_head, count_tm, blocks, part, heads, block, total_blocks, slots, padded, grouped = sizes
    pairs = (key_ref, value_ref)
    pair_heads, query_heads = grouped
    pair_groups, query_groups = heads // pair_heads, heads // query_heads
    offsets = range(1, count_tm)
    places = {o: [p for k, p in slots if k == o] for o in offsets}
    width = heads * HD
    my_head = lax.axis_index("head")
    me = lax.axis_index("tm")
    scale = 1.0 / math.sqrt(HD)
    slot_of = {slot: i for i, slot in enumerate(slots)}
    others = [k + jnp.where(my_head <= k, 1, 0) for k in range(count_head - 1)]
    upper_half = my_head >= count_head // 2
    far_first = [
        jnp.where(upper_half, low, high) for low, high in zip(others, reversed(others))
    ]

    def columns_of(owner, first, count):
        return pl.ds(pl.multiple_of(owner * width + first * HD, HD), count * HD)

    def head_copy(is_query, peer, g, source=None):
        source = my_head if source is None else source
        if is_query:
            sent = query_ref.at[:, :, columns_of(peer, g * query_heads, query_heads)]
            landing = query_in.at[g, source]
        else:
            sent, landing = packed.at[g, peer], pair_in.at[g, source]
        return pltpu.make_async_remote_copy(
            src_ref=sent,
            dst_ref=landing,
            send_sem=head_send.at[is_query, peer, g],
            recv_sem=head_recv.at[is_query, source, g],
            device_id={"head": peer},
            device_id_type=MESH,
        )

    def pair_columns(which, owner, g):
        return pairs[which].at[:, :, columns_of(owner, g * pair_heads, pair_heads)]

    def pack_copy(which, peer, g):
        return pltpu.make_async_copy(
            pair_columns(which, peer, g), packed.at[g, peer, which], pack_sem.at[which, peer, g]
        )

    def own_pair(which, g):
        return pltpu.make_async_copy(
            pair_columns(which, my_head, g),
            pair_in.at[g, my_head, which],
            pair_local.at[which, g],
        )

    def own_query(g):
        return pltpu.make_async_copy(
            query_ref.at[:, :, columns_of(my_head, g * query_heads, query_heads)],
            query_in.at[g, my_head],
            query_local.at[g],
        )

    def halo_copy(g, offset, count, arriving=False):
        peer = lax.rem(me + offset, count_tm)
        first = slot_of[(offset, 0)]
        landing = first if arriving else slot_of[(count_tm - offset, 0)]
        return pltpu.make_async_remote_copy(
            src_ref=outbox.at[g, pl.ds(first, count)],
            dst_ref=halo.at[g, pl.ds(landing, count)],
            send_sem=halo_send.at[g, offset - 1],
            recv_sem=halo_recv.at[g, (offset if arriving else count_tm - offset) - 1],
            device_id={"tm": peer},
            device_id_type=MESH,
        )

    def beside(offset):
        peer = lax.rem(me + offset, count_tm)
        return (peer == me + 1) | (peer == me - 1)

    def each_halo(g, action, arriving=False):
        for offset in offsets:
            full = len(places[offset])
            if full == FAR_CAP:
                action(halo_copy(g, offset, full, arriving))
            else:
                near = beside(offset)
                pl.when(near)(lambda o=offset, n=full: action(halo_copy(g, o, n, arriving)))
                pl.when(jnp.logical_not(near))(
                    lambda o=offset: action(halo_copy(g, o, FAR_CAP, arriving))
                )

    def back_copy(peer, g, source=None):
        source = my_head if source is None else source
        return pltpu.make_async_remote_copy(
            src_ref=staged.at[g, peer],
            dst_ref=out_ref.at[:, :, columns_of(source, g * query_heads, query_heads)],
            send_sem=back_send.at[peer, g],
            recv_sem=back_recv.at[source, g],
            device_id={"head": peer},
            device_id_type=MESH,
        )

    def back_own(g):
        return pltpu.make_async_copy(
            staged.at[g, my_head],
            out_ref.at[:, :, columns_of(my_head, g * query_heads, query_heads)],
            back_local.at[g],
        )

    def greet(axis, peer):
        pl.semaphore_signal(
            pltpu.get_barrier_semaphore(), inc=1, device_id={axis: peer}, device_id_type=MESH
        )

    def tell(semaphore, peer):
        pl.semaphore_signal(semaphore, inc=1, device_id={"head": peer}, device_id_type=MESH)

    has_low, has_high = my_head > 0, my_head < count_head - 1
    pl.when(has_low)(lambda: greet("head", my_head - 1))
    pl.when(has_high)(lambda: greet("head", my_head + 1))
    hub = my_head == 0

    @pl.when(hub)
    def _():
        for offset in range(1, count_tm):
            greet("tm", lax.rem(me + offset, count_tm))

    pair_copy = pltpu.make_async_copy(pair_ref, pair_here, pair_sem)
    pair_copy.start()
    tokens_copy = pltpu.make_async_copy(tokens_far, tokens_ref, tokens_sem)
    tokens_copy.start()
    for g in range(pair_groups):
        for peer in others:
            for which in range(2):
                pack_copy(which, peer, g).start()
        for which in range(2):
            own_pair(which, g).start()
    for g in range(query_groups):
        own_query(g).start()

    def clear(i):
        halo[:, i] = jnp.zeros((pair_groups, 2, pair_heads, block, HD), jnp.bfloat16)

    for i, (offset, place) in enumerate(slots):
        if place >= FAR_CAP:
            pl.when(jnp.logical_not(beside(offset)))(lambda i=i: clear(i))
    sign_ref[...] = sign_table(HD).astype(jnp.bfloat16)

    neighbours = jnp.where(has_low, 1, 0) + jnp.where(has_high, 1, 0)
    awaited = neighbours + jnp.where(hub, count_tm - 1, 0)
    pl.semaphore_wait(pltpu.get_barrier_semaphore(), awaited)

    pieces = [(0, g) for g in range(pair_groups)] + [(1, g) for g in range(query_groups)]
    early = pieces[: min(EARLY, pair_groups)]
    for _, g in early:
        for peer in others:
            for which in range(2):
                pack_copy(which, peer, g).wait()

    def start_at(distance):
        for side in (-distance, distance):
            peer = my_head + side
            inside = (peer >= 0) & (peer < count_head)
            for kind, g in early:
                pl.when(inside)(lambda p=peer, k=kind, g=g: head_copy(k, p, g).start())

    for distance in range(1, count_head):
        if distance > 1:
            seen_low, seen_high = my_head >= distance - 1, my_head <= count_head - distance
            low, high = entered_low.at[distance - 2], entered_high.at[distance - 2]
            pl.when(seen_low & has_high)(lambda low=low: tell(low, my_head + 1))
            pl.when(seen_high & has_low)(lambda high=high: tell(high, my_head - 1))
            pl.when(my_head >= distance)(lambda low=low: pl.semaphore_wait(low, 1))
            pl.when(my_head <= count_head - 1 - distance)(
                lambda high=high: pl.semaphore_wait(high, 1)
            )
        start_at(distance)
    pl.when(my_head < count_head - 1)(lambda: pl.semaphore_wait(column_up, 1))
    pl.when(has_low)(lambda: tell(column_up, my_head - 1))

    for kind, g in pieces:
        if (kind, g) not in early:
            for peer in far_first:
                if kind == 0:
                    for which in range(2):
                        pack_copy(which, peer, g).wait()
                head_copy(kind, peer, g).start()

    @pl.when(hub)
    def _():
        for offset in range(1, count_tm):
            pl.semaphore_signal(
                column_side,
                inc=1,
                device_id={"tm": lax.rem(me + offset, count_tm)},
                device_id_type=MESH,
            )

    pair_copy.wait()
    tokens_copy.wait()
    listing = pair_here[...]
    lane = lax.broadcasted_iota(jnp.int32, (1, LANES), 1)
    listed = jnp.zeros((total_blocks, LANES), jnp.float32)
    token_row = jnp.zeros((1, LANES), jnp.float32)
    for k in range(total_blocks):
        found = jnp.max(jnp.where(listing == k, 1.0, 0.0), axis=1, keepdims=True)
        here = jnp.where(lane == k, 1.0, 0.0)
        listed = listed + found * here
        token_row = token_row + here * tokens_ref[k].astype(jnp.float32)
    wanted_ref[...] = jnp.zeros_like(wanted_ref)
    for t in range(count_tm):
        of_shard = listed[t * blocks : (t + 1) * blocks]
        listed_ref[t] = of_shard
        wanted_ref[t : t + 1, :] = jnp.max(of_shard, axis=0, keepdims=True)
    low = lax.broadcasted_iota(jnp.int32, (LANES, LANES), 0)
    high = lax.broadcasted_iota(jnp.int32, (LANES, LANES), 1)
    low_shard, high_shard = jnp.zeros_like(low), jnp.zeros_like(high)
    lane_shard = jnp.zeros_like(lane)
    for t in range(1, count_tm):
        low_shard = low_shard + jnp.where(low >= t * blocks, 1, 0)
        high_shard = high_shard + jnp.where(high >= t * blocks, 1, 0)
        lane_shard = lane_shard + jnp.where(lane >= t * blocks, 1, 0)
    before = jnp.where((low_shard == high_shard) & (low < high), 1.0, 0.0).astype(jnp.bfloat16)
    wanted = wanted_ref[...]
    rank = jnp.dot(wanted.astype(jnp.bfloat16), before, preferred_element_type=jnp.float32)
    for place in range(NEAR_CAP):
        chosen = jnp.where(rank == float(place), wanted, 0.0)
        for t in range(count_tm):
            place_ref[place, t] = chosen[t : t + 1, :]
    picks = []
    for offset, place in slots:
        row = place_ref[place, lax.rem(me + offset, count_tm)]
        picks.append(
            [
                jnp.sum(jnp.where(lane == me * blocks + j, row, 0.0), axis=1, keepdims=True)
                for j in range(blocks)
            ]
        )
    mine = listed_ref[me]
    key_lane = lax.broadcasted_iota(jnp.int32, (1, padded * block), 1)
    key_end = jnp.zeros((blocks, padded * block), jnp.float32)
    for i in range(blocks + len(slots)):
        if i < blocks:
            kept_tokens = jnp.where(lane == me * blocks + i, token_row, 0.0)
        else:
            offset, place = slots[i - blocks]
            owner = lax.rem(me + offset, count_tm)
            row = place_ref[place, me]
            kept_tokens = jnp.where(lane_shard == owner, row * token_row, 0.0)
        kept = jnp.sum(mine * kept_tokens, axis=1, keepdims=True)
        inside = jnp.where((key_lane >= i * block) & (key_lane < (i + 1) * block), 1.0, 0.0)
        key_end = key_end + inside * (kept + float(i * block))
    bias_ref[...] = jnp.where(key_lane.astype(jnp.float32) < key_end, 0.0, -1e30)

    def arrived(kind, g):
        for peer in others:
            head_copy(kind, peer, g, source=peer).wait_recv()

    def rotated(landed, column):
        lanes = pl.ds(pl.multiple_of(column * HD, HD), HD)
        rows = jnp.concatenate(
            [landed[:, b, :, lanes].astype(jnp.float32).reshape(block, HD) for b in range(blocks)],
            axis=0,
        ).astype(jnp.bfloat16)
        turned = jnp.dot(rows, sign_ref[...], preferred_element_type=jnp.float32) * scale
        return turned.astype(jnp.bfloat16)

    def spread(g, carry):
        for which in range(2):
            own_pair(which, g).wait()
        arrived(0, g)

        def one_head(column, carry):
            for which in range(2):
                turned = rotated(pair_in.at[g, :, which], column)
                store[which, g * pair_heads + column] = turned
                wide = turned.astype(jnp.float32)
                for i in range(len(slots)):
                    sent = picks[i][0] * wide[0:block]
                    for j in range(1, blocks):
                        sent = sent + picks[i][j] * wide[j * block : (j + 1) * block]
                    outbox[g, i, which, column] = sent.astype(jnp.bfloat16)
            return carry

        lax.fori_loop(0, pair_heads, one_head, 0)
        each_halo(g, lambda copy: copy.start())
        return carry

    position = lax.broadcasted_iota(jnp.int32, (block, HD), 0)
    spare = padded - blocks - len(slots)

    to_base_two = scale * math.log2(math.e)

    def listed_rows(which, h):
        pieces = [store[which, h]]
        for i in range(len(slots)):
            pieces.append(halo[lax.div(h, pair_heads), i, which, lax.rem(h, pair_heads)])
        if spare > 0:
            pieces.append(jnp.zeros((spare * block, HD), jnp.bfloat16))
        return jnp.concatenate(pieces, axis=0)

    def softmax(scores):
        halves, denominators = [], []
        for b in range(blocks):
            of_block = scores[b * block : (b + 1) * block] + bias_ref[b : b + 1, :]
            peak = jnp.max(of_block, axis=1, keepdims=True)
            weights = jnp.exp2((of_block - peak) * to_base_two)
            denominators.append(jnp.sum(weights, axis=1, keepdims=True))
            halves.append(weights.astype(jnp.bfloat16))
        return jnp.concatenate(halves, axis=0), 1.0 / jnp.concatenate(denominators, axis=0)

    def turned_back(mixed):
        first = mixed.astype(jnp.bfloat16)
        rest = mixed - first.astype(jnp.float32)
        second = rest.astype(jnp.bfloat16)
        third = (rest - second.astype(jnp.float32)).astype(jnp.bfloat16)
        sign = sign_ref[...]
        turned = jnp.dot(
            jnp.concatenate([first, second], axis=1),
            jnp.concatenate([sign, sign], axis=0),
            preferred_element_type=jnp.float32,
        )
        return (turned + jnp.dot(third, sign, preferred_element_type=jnp.float32)) * scale

    def attend(g):
        columns = range(query_heads)
        queries = [rotated(query_in.at[g], column) for column in columns]
        scores = [
            lax.dot_general(
                queries[column],
                listed_rows(0, g * query_heads + column),
                (((1,), (1,)), ((), ())),
                preferred_element_type=jnp.float32,
            )
            for column in columns
        ]
        weighted = [softmax(of_head) for of_head in scores]
        mixed = [
            jnp.dot(
                weighted[column][0],
                listed_rows(1, g * query_heads + column),
                preferred_element_type=jnp.float32,
            )
            * weighted[column][1]
            for column in columns
        ]
        results = [turned_back(of_head) for of_head in mixed]
        for b in range(blocks):
            live = position < tokens_ref[me * blocks + b]
            for column in columns:
                result = jnp.where(live, results[column][b * block : (b + 1) * block], 0.0)
                for owner in range(count_head):
                    staged[g, owner, b, :, column * HD : (column + 1) * HD] = result[
                        owner * part : (owner + 1) * part
                    ].astype(jnp.bfloat16)

    pl.when(hub)(lambda: pl.semaphore_wait(column_side, count_tm - 1))
    pl.when(has_low)(lambda: pl.semaphore_wait(column_down, 1))
    pl.when(has_high)(lambda: tell(column_down, my_head + 1))
    lax.fori_loop(0, pair_groups, spread, 0)

    def attend_group(g, carry):
        own_query(g).wait()
        arrived(1, g)
        for j in range(pair_groups):
            first = j * pair_heads - g * query_heads
            pl.when((first >= 0) & (first < query_heads))(
                lambda j=j: each_halo(j, lambda copy: copy.wait_recv(), arriving=True)
            )
        attend(g)
        for peer in far_first:
            now = jnp.logical_not(deferred(peer))
            pl.when(now)(lambda peer=peer: back_copy(peer, g).start())
        back_own(g).start()
        pl.when(g >= DEFER)(lambda: send_deferred(g - DEFER))
        return carry

    def deferred(peer):
        beside_me = (peer == my_head + 1) | (peer == my_head - 1)
        return (my_head > 0) & (peer > 0) & beside_me

    def send_deferred(g):
        for peer in far_first:
            pl.when(deferred(peer))(lambda peer=peer: back_copy(peer, g).start())

    lax.fori_loop(0, query_groups, attend_group, 0)
    for g in range(max(0, query_groups - DEFER), query_groups):
        send_deferred(g)

    for kind, g in pieces:
        for peer in others:
            head_copy(kind, peer, g).wait_send()
        if kind == 0:
            each_halo(g, lambda copy: copy.wait_send())
    for g in range(query_groups):
        for peer in others:
            back_copy(peer, g).wait_send()
            back_copy(peer, g, source=peer).wait_recv()
        back_own(g).wait()


def shards(query_rows, key_rows, value_rows, pair_list, block_tokens):
    count_head = lax.axis_size("head")
    count_tm = lax.axis_size("tm")
    blocks, part, full_width = query_rows.shape
    block = part * count_head
    heads = full_width // (HD * count_head)
    total_blocks, listed = pair_list.shape
    slots = incoming_slots(count_tm)
    filled = blocks + len(slots)
    per_lane_tile = max(1, LANES // block)
    padded = -(-filled // per_lane_tile) * per_lane_tile
    shard_rows = -(-count_tm // 8) * 8
    pair_heads = heads_together(heads, PAIR_HEADS)
    query_heads = heads_together(heads, QUERY_HEADS)
    grouped = (pair_heads, query_heads)
    pair_groups, query_groups = [heads // size for size in grouped]
    most = max(pair_groups, query_groups)
    pair_shape = (pair_groups, count_head, 2, blocks, part, pair_heads * HD)
    query_shape = (query_groups, count_head, blocks, part, query_heads * HD)
    halo_shape = (pair_groups, len(slots), 2, pair_heads, block, HD)
    sizes = (
        count_head, count_tm, blocks, part, heads, block, total_blocks, slots, padded, grouped
    )
    rounds = max(1, count_head - 2)
    in_hbm = pl.BlockSpec(memory_space=pltpu.HBM)
    dma = pltpu.SemaphoreType.DMA
    return pl.pallas_call(
        functools.partial(kernel, sizes),
        out_shape=jax.ShapeDtypeStruct(query_rows.shape, jnp.bfloat16),
        in_specs=[in_hbm] * 5,
        out_specs=in_hbm,
        scratch_shapes=[
            pltpu.VMEM(pair_shape, jnp.bfloat16),
            pltpu.VMEM(pair_shape, jnp.bfloat16),
            pltpu.VMEM(query_shape, jnp.bfloat16),
            pltpu.VMEM((2, heads, blocks * block, HD), jnp.bfloat16),
            pltpu.VMEM(halo_shape, jnp.bfloat16),
            pltpu.VMEM(halo_shape, jnp.bfloat16),
            pltpu.VMEM(query_shape, jnp.bfloat16),
            pltpu.VMEM((total_blocks, listed), jnp.int32),
            pltpu.SMEM((total_blocks,), jnp.int32),
            pltpu.VMEM((count_tm, blocks, LANES), jnp.float32),
            pltpu.VMEM((NEAR_CAP, count_tm, 1, LANES), jnp.float32),
            pltpu.VMEM((shard_rows, LANES), jnp.float32),
            pltpu.VMEM((blocks, padded * block), jnp.float32),
            pltpu.VMEM((HD, HD), jnp.bfloat16),
            dma((2, count_head, most)),
            dma((2, count_head, most)),
            dma((2, pair_groups)),
            dma((query_groups,)),
            dma((2, count_head, pair_groups)),
            pltpu.SemaphoreType.REGULAR((rounds,)),
            pltpu.SemaphoreType.REGULAR((rounds,)),
            pltpu.SemaphoreType.REGULAR,
            pltpu.SemaphoreType.REGULAR,
            pltpu.SemaphoreType.REGULAR,
            dma((pair_groups, count_tm - 1)),
            dma((pair_groups, count_tm - 1)),
            dma((count_head, query_groups)),
            dma((count_head, query_groups)),
            dma((query_groups,)),
            dma(()),
            dma(()),
        ],
        compiler_params=pltpu.CompilerParams(
            collective_id=0,
            has_side_effects=True,
            vmem_limit_bytes=32 * 1024 * 1024,
        ),
    )(*[pltpu.with_memory_space_constraint(x, pltpu.HBM) for x in (query_rows, key_rows, value_rows, pair_list, block_tokens)])


def solution(mesh):
    placed = (
        P(("grp", "tm"), "head", None),
        P(("grp", "tm"), "head", None),
        P(("grp", "tm"), "head", None),
        P("grp", None),
        P("grp"),
    )
    return jax.shard_map(
        shards,
        mesh=mesh,
        in_specs=placed,
        out_specs=P(("grp", "tm"), "head", None),
        check_vma=False,
    )
```
